32 devices in a mesh: rep: 2 (over x), node: 16 (over z, y, core).
Axes of the slice: x: 2, y: 2, z: 4, core: 2. Of those that a mesh axis runs over, the one named last changes fastest.
Arguments:
- tokens: bfloat16 [4096, 7168], P(('rep', 'node')), parts along dimension 0, may hold values from -6 to 6
- group_choice: int32 [4096, 4], P(('rep', 'node')), parts along dimension 0, may hold values from 0 to 7, as said below
- expert_picks: int32 [4096, 8], P(('rep', 'node')), parts along dimension 0, may hold values from 0 to 255, as said below
- gate_fixed: int32 [4096, 8], P(('rep', 'node')), parts along dimension 0, may hold values from 1 to 65535
- token_counts: int32 [32], P(('rep', 'node')), parts along dimension 0, may hold values from 16 to 128, as said below
- expert_gate: bfloat16 [7168, 2048], P(None, 'node'), may hold values from -0.0625 to 0.0625
- expert_up: bfloat16 [7168, 2048], P(None, 'node'), may hold values from -0.0625 to 0.0625
- expert_down: bfloat16 [2048, 7168], P('node'), may hold values from -0.1875 to 0.1875
Outputs:
- routed_out: bfloat16 [4096, 7168], P(('rep', 'node')), parts along dimension 0
The draws below stay inside these ranges and needn't reach their ends.
There are 2 independent parts, one for each index of `rep`. The reference program is written for one: setup_inputs(seed, part) draws one part's arguments, and reference() takes and returns one part's arrays. A program takes and returns all parts, laid end to end along the dimension named above; an argument that names none is the same for every part. Nothing has to cross between parts.
Inputs may be any that keep to these rules, and one draw needn't show every extreme that they name: `group_choice`: each row holds 4 different groups. `expert_picks`: each row names 8 different experts, two from each group of the same row of group_choice (expert e lies in group e // 32); at most one of them is a held expert f * 32 with f < 2. Among the valid tokens of one device each held expert is picked at most 8 times, and in every draw one held expert is picked exactly 8 times on every device. `token_counts`: some device has 128 valid tokens and some device 2 * 8.
All inputs are finite; a program needn't handle non-finite values.
Results may differ from the reference program's by a relative error of at most 0.0064.
Values may be sent and summed in bfloat16 or wider, within the bound.
No kernel may reach another device: no remote copies, remote signals or barrier semaphores. Data moves between devices by JAX's collectives and lax.ppermute only.
A program may use at most 64 MiB of HBM per device.

```python
import jax
import jax.numpy as jnp

D = 7168
FFW = 1024
GROUPS = 8
TOPG = 4
TOPK = 8
SPLIT = 8
TOK_DEV = 128
GROUP_SIZE = 32
HID = 128
FLIGHT = 2
CAP = 8
TOKENS = 2048


def routing_tables(key):
    dev_count = TOKENS // TOK_DEV
    subkeys = [jax.random.fold_in(key, 7001 + number) for number in range(12)]
    base_counts = jax.random.randint(subkeys[0], (dev_count,), FLIGHT * CAP, TOK_DEV + 1)
    dev_order = jax.random.permutation(subkeys[1], dev_count)
    dev_ids = jnp.arange(dev_count)
    token_counts = jnp.where(dev_ids == dev_order[0], TOK_DEV, base_counts)
    token_counts = jnp.where(dev_ids == dev_order[1], FLIGHT * CAP, token_counts)
    heavy_caps = jax.random.randint(subkeys[2], (FLIGHT,), 1, CAP + 1)
    load_sizes = jax.random.randint(subkeys[3], (dev_count, FLIGHT), 0, 1 << 16) % heavy_caps[None, :] + 1
    chosen = jax.random.randint(subkeys[4], (), 0, FLIGHT)
    load_sizes = jnp.where(jnp.arange(FLIGHT)[None, :] == chosen, CAP, load_sizes)
    local_ids = jnp.arange(TOK_DEV)
    scores = jax.random.randint(subkeys[5], (dev_count, TOK_DEV), 0, 1 << 16) * TOK_DEV + local_ids[None, :]
    scores = scores + jnp.where(local_ids[None, :] >= token_counts[:, None], (1 << 16) * TOK_DEV, 0)
    token_rank = jnp.argsort(jnp.argsort(scores, axis=1), axis=1)
    load_ends = jnp.cumsum(load_sizes, axis=1)
    starts = load_ends - load_sizes
    inside = (token_rank[:, :, None] >= starts[:, None, :]) & (token_rank[:, :, None] < load_ends[:, None, :])
    has_flight = jnp.any(inside, axis=2)
    flight_id = jnp.sum(jnp.where(inside, jnp.arange(FLIGHT)[None, None, :], 0), axis=2)
    invalid_slot = local_ids[None, :] >= token_counts[:, None]
    extra_pick = jax.random.randint(subkeys[11], (dev_count, TOK_DEV), 0, 2 * FLIGHT)
    invalid_held = invalid_slot & (extra_pick < FLIGHT)
    has_flight = (has_flight | invalid_held).reshape(TOKENS)
    flight_id = jnp.where(invalid_held, extra_pick, flight_id).reshape(TOKENS)
    group_score = jax.random.randint(subkeys[6], (TOKENS, GROUPS), 0, 1 << 16) * GROUPS + jnp.arange(GROUPS)[None, :]
    group_score = jnp.where(has_flight[:, None] & (jnp.arange(GROUPS)[None, :] == flight_id[:, None]), -1, group_score)
    groups = jnp.argsort(group_score, axis=1)[:, :TOPG]
    first_off = jax.random.randint(subkeys[7], (TOKENS, TOPG), 1, GROUP_SIZE)
    second = 1 + (first_off - 1 + jax.random.randint(subkeys[8], (TOKENS, TOPG), 1, GROUP_SIZE - 1)) % (GROUP_SIZE - 1)
    first_off = jnp.where((jnp.arange(TOPG)[None, :] == 0) & has_flight[:, None], 0, first_off)
    picked_experts = jnp.stack([groups * GROUP_SIZE + first_off, groups * GROUP_SIZE + second], axis=2).reshape(TOKENS, TOPK)
    column_score = jax.random.randint(subkeys[9], (TOKENS, TOPK), 0, 1 << 16) * TOPK + jnp.arange(TOPK)[None, :]
    picked_experts = jnp.take_along_axis(picked_experts, jnp.argsort(column_score, axis=1), axis=1)
    group_order = jax.random.randint(subkeys[10], (TOKENS, TOPG), 0, 1 << 16) * TOPG + jnp.arange(TOPG)[None, :]
    groups = jnp.take_along_axis(groups, jnp.argsort(group_order, axis=1), axis=1)
    return (token_counts.astype(jnp.int32), groups.astype(jnp.int32), picked_experts.astype(jnp.int32))


def draw_token_counts(key, part):
    return routing_tables(key)[0]


def draw_group_choice(key, part):
    return routing_tables(key)[1]


def draw_expert_picks(key, part):
    return routing_tables(key)[2]


def plant(values, rng, low, top_value):
    index_at = [jax.random.randint(jax.random.fold_in(rng, axis), (), 0, length) for axis, length in enumerate(values.shape)]
    widest = values.shape.index(max(values.shape))
    next_to = index_at[:widest] + [(index_at[widest] + 1) % values.shape[widest]] + index_at[widest + 1:]
    return values.at[tuple(index_at)].set(low).at[tuple(next_to)].set(top_value)


def levels(rng, extent, shards, low, high):
    def one(dim, shards_of):
        steps = jax.random.uniform(jax.random.fold_in(jax.random.fold_in(rng, 6), dim), (shards_of,), jnp.float32, low / len(shards), high / len(shards))
        return jnp.repeat(jnp.exp(steps), extent[dim] // shards_of).reshape((-1,) + (1,) * (len(extent) - dim - 1))

    loudness = one(*shards[0])
    for cut in shards[1:]:
        loudness = loudness * one(*cut)
    return loudness


def bell_draw(rng, extent, width, reach, cuts=(), held_as=jnp.bfloat16):
    factor_of = levels(rng, extent, cuts, -0.22, 0.18) if cuts else 1.0
    array = jax.random.normal(rng, extent, jnp.float32) * width * factor_of
    return jnp.minimum(jnp.maximum(array, -reach), reach).astype(held_as)


def setup_inputs(seed: int = 0, part: int = 0) -> dict:
    key_of = jax.random.split(jax.random.key(seed), 9)
    part_keys = jax.random.split(jax.random.fold_in(key_of[8], part), 9)
    return {
        "tokens": bell_draw(part_keys[0], (TOKENS, D), 1.0, 6.0, ((0, 16),)),
        "group_choice": draw_group_choice(jax.random.fold_in(jax.random.fold_in(key_of[8], part), 71), part),
        "expert_picks": draw_expert_picks(jax.random.fold_in(jax.random.fold_in(key_of[8], part), 71), part),
        "gate_fixed": plant(jax.random.randint(part_keys[3], (TOKENS, TOPK), 1, 65536), jax.random.fold_in(part_keys[3], 1), 1, 65535).astype(jnp.int32),
        "token_counts": draw_token_counts(jax.random.fold_in(jax.random.fold_in(key_of[8], part), 71), part),
        "expert_gate": bell_draw(key_of[5], (D, FLIGHT * FFW), D ** -0.5, 0.0625, ((1, 16),)),
        "expert_up": bell_draw(key_of[6], (D, FLIGHT * FFW), D ** -0.5, 0.0625, ((1, 16),)),
        "expert_down": bell_draw(key_of[7], (FLIGHT * FFW, D), FFW ** -0.5, 0.1875, ((0, 16),)),
    }


def expert_output(rows_in, expert_gate, expert_up, expert_down, expert):
    total = jnp.zeros((rows_in.shape[0], expert_down.shape[1]), jnp.float32)
    for member in range(SPLIT):
        column = (expert * SPLIT + member) * HID
        gate_val = jnp.dot(rows_in, expert_gate[:, column:column + HID], preferred_element_type=jnp.float32)
        up_val = jnp.dot(rows_in, expert_up[:, column:column + HID], preferred_element_type=jnp.float32)
        hidden = (jax.nn.silu(gate_val) * up_val).astype(jnp.bfloat16)
        partial_out = jnp.dot(hidden, expert_down[column:column + HID, :], preferred_element_type=jnp.float32).astype(jnp.bfloat16)
        total = total + partial_out.astype(jnp.float32)
    return total.astype(jnp.bfloat16)


def reference(tokens, group_choice, expert_picks, gate_fixed, token_counts, expert_gate, expert_up, expert_down):
    total_rows = tokens.shape[0]
    position = jnp.arange(total_rows, dtype=jnp.int32)
    device_of = position // TOK_DEV
    is_valid = (position % TOK_DEV) < token_counts[device_of]
    gate_vals = gate_fixed.astype(jnp.float32)
    weight = 2.5 * gate_vals / jnp.sum(gate_vals, axis=1, keepdims=True)
    in_group = jnp.any((expert_picks // GROUP_SIZE)[:, :, None] == group_choice[:, None, :], axis=2)
    counted = in_group & is_valid[:, None]
    result = jnp.zeros(tokens.shape, jnp.float32)
    capacity = (total_rows // TOK_DEV) * CAP
    for expert in range(FLIGHT):
        matches = counted & (expert_picks == expert * GROUP_SIZE)
        picked = jnp.any(matches, axis=1)
        shares = jnp.sum(jnp.where(matches, weight, 0.0), axis=1)
        chosen = jnp.argsort(jnp.where(picked, 0, 1).astype(jnp.int32), stable=True)[:capacity].astype(jnp.int32)
        outputs = expert_output(tokens[chosen], expert_gate, expert_up, expert_down, expert)
        result = result.at[chosen].add(outputs.astype(jnp.float32) * shares[chosen][:, None])
    return result.astype(jnp.bfloat16)
```

```python
import functools

import jax
import jax.numpy as jnp
from jax import lax
from jax.experimental import pallas as pl
from jax.experimental.pallas import tpu as pltpu
from jax.sharding import PartitionSpec as P

SPLIT = 8
GROUP_SIZE = 32
SCALE = 2.5
CORES = 2
CHIPS = SPLIT // CORES

VMEM = pl.BlockSpec(memory_space=pltpu.VMEM)
SMEM = pl.BlockSpec(memory_space=pltpu.SMEM)
ANY = pl.BlockSpec(memory_space=pl.ANY)


def column_step(width, limit):
    step = limit
    while width % step:
        step -= 128
    return step


def route_kernel(
    flight,
    capacity,
    me_ref,
    count_ref,
    groups_ref,
    picks_ref,
    gate_ref,
    tokens_ref,
    *refs,
):
    row_refs = refs[:flight]
    select_ref, share_ref, held, sem = refs[flight:]
    load = pltpu.make_async_copy(tokens_ref, held, sem)
    load.start()
    picks = picks_ref[...]
    groups = groups_ref[...]
    row_count = picks.shape[1]
    lanes = lax.broadcasted_iota(jnp.int32, (1, row_count), 1)
    picked_group = lax.shift_right_logical(picks, GROUP_SIZE.bit_length() - 1)
    counted = picked_group == groups[0:1, :]
    for place in range(1, groups.shape[0]):
        counted = counted | (picked_group == groups[place : place + 1, :])
    counted = counted & (lanes < count_ref[0])
    gate_vals = gate_ref[...].astype(jnp.float32)
    weight = SCALE * gate_vals / jnp.sum(gate_vals, axis=0, keepdims=True)
    rows_of = lax.broadcasted_iota(jnp.int32, (row_count, row_count), 0)
    cols_of = lax.broadcasted_iota(jnp.int32, (row_count, row_count), 1)
    upto = (rows_of <= cols_of).astype(jnp.bfloat16)
    slots = lax.broadcasted_iota(jnp.int32, (capacity, row_count), 0)
    selects = []
    for step in range(flight):
        expert = lax.rem(me_ref[0] + step, flight)
        match = counted & (picks == expert * GROUP_SIZE)
        picked = jnp.max(match.astype(jnp.float32), axis=0, keepdims=True)
        share = jnp.sum(jnp.where(match, weight, 0.0), axis=0, keepdims=True)
        rank = jnp.dot(
            jnp.broadcast_to(picked, (capacity, row_count)).astype(jnp.bfloat16),
            upto,
            preferred_element_type=jnp.float32,
        )
        hit = (picked > 0.5) & (rank.astype(jnp.int32) - 1 == slots)
        selects.append(jnp.where(hit, 1.0, 0.0))
        slot_share = jnp.sum(jnp.where(hit, share, 0.0), axis=1, keepdims=True)
        share_ref[step * capacity : (step + 1) * capacity, :] = jnp.broadcast_to(
            slot_share, (capacity, share_ref.shape[1])
        )
    select = jnp.concatenate(selects, axis=0).astype(jnp.bfloat16)
    select_ref[...] = select
    load.wait()
    width = held.shape[1]
    span = column_step(width, 1024)
    for start in range(0, width, span):
        rows = jnp.dot(
            select, held[:, start : start + span], preferred_element_type=jnp.float32
        ).astype(jnp.bfloat16)
        for step in range(flight):
            row_refs[step][:, start : start + span] = rows[
                step * capacity : (step + 1) * capacity
            ]


def route(me, counts, groups, picks, gate, tokens, flight, capacity):
    row_count, width = tokens.shape
    return pl.pallas_call(
        functools.partial(route_kernel, flight, capacity),
        out_shape=[jax.ShapeDtypeStruct((capacity, width), jnp.bfloat16)] * flight
        + [
            jax.ShapeDtypeStruct((flight * capacity, row_count), jnp.bfloat16),
            jax.ShapeDtypeStruct((flight * capacity, 128), jnp.float32),
        ],
        in_specs=[SMEM, SMEM, VMEM, VMEM, VMEM, ANY],
        out_specs=[VMEM] * (flight + 2),
        scratch_shapes=[
            pltpu.VMEM((row_count, width), jnp.bfloat16),
            pltpu.SemaphoreType.DMA,
        ],
        compiler_params=pltpu.CompilerParams(vmem_limit_bytes=16 << 20),
        cost_estimate=pl.CostEstimate(
            flops=2 * flight * capacity * row_count * width,
            bytes_accessed=2 * row_count * width,
            transcendentals=0,
        ),
        name="route",
    )(me, counts, groups, picks, gate, tokens)


def ffn_kernel(blocks, *refs):
    in_refs = refs[:blocks]
    gate_refs = refs[blocks : blocks + CORES]
    up_refs = refs[blocks + CORES : blocks + 2 * CORES]
    down_refs = refs[blocks + 2 * CORES : blocks + 3 * CORES]
    out_refs = refs[blocks + 3 * CORES :]
    rows, width = in_refs[0].shape
    hid = gate_refs[0].shape[1]
    span = column_step(width, 1024)
    totals = [jnp.zeros((blocks * rows, 2 * hid), jnp.float32)] * CORES
    for start in range(0, width, span):
        part = slice(start, start + span)
        x = jnp.concatenate([ref[:, part] for ref in in_refs], axis=0)
        for core in range(CORES):
            both = jnp.concatenate([gate_refs[core][part, :], up_refs[core][part, :]], axis=1)
            totals[core] = totals[core] + jnp.dot(x, both, preferred_element_type=jnp.float32)
    hidden = []
    for total in totals:
        gate_val, up_val = total[:, :hid], total[:, hid:]
        hidden.append((gate_val / (1.0 + jnp.exp(-gate_val)) * up_val).astype(jnp.bfloat16))
    hidden = jnp.concatenate(hidden, axis=1)
    for start in range(0, width, span):
        part = slice(start, start + span)
        down = jnp.concatenate([ref[:, part] for ref in down_refs], axis=0)
        out = jnp.dot(hidden, down, preferred_element_type=jnp.float32).astype(jnp.bfloat16)
        for block in range(blocks):
            out_refs[block][:, part] = out[block * rows : (block + 1) * rows]


def ffn(xs, gates, ups, downs):
    blocks = len(xs)
    rows, width = xs[0].shape
    hid = gates[0].shape[1]
    return pl.pallas_call(
        functools.partial(ffn_kernel, blocks),
        out_shape=[jax.ShapeDtypeStruct((rows, width), jnp.bfloat16)] * blocks,
        in_specs=[VMEM] * (blocks + 3 * CORES),
        out_specs=[VMEM] * blocks,
        compiler_params=pltpu.CompilerParams(vmem_limit_bytes=30 << 20),
        cost_estimate=pl.CostEstimate(
            flops=2 * blocks * rows * width * hid * 3 * CORES,
            bytes_accessed=2 * 3 * CORES * width * hid,
            transcendentals=0,
        ),
        name="ffn",
    )(*xs, *gates, *ups, *downs)


def finish_kernel(flight, capacity, select_ref, share_ref, *refs):
    near_refs = refs[:CHIPS]
    far_refs = refs[CHIPS : CHIPS + flight - 1]
    out_ref, held, sems = refs[CHIPS + flight - 1 :]
    width = held.shape[1]
    span = column_step(width, 1024)
    select = select_ref[...]
    copies = []
    for place, start in enumerate(range(0, width, span)):
        part = slice(start, start + span)
        near = near_refs[0][:, part].astype(jnp.float32)
        for ref in near_refs[1:]:
            near = near + ref[:, part].astype(jnp.float32)
        near = near.astype(jnp.bfloat16).astype(jnp.float32)
        far = [ref[:, part].astype(jnp.float32) for ref in far_refs]
        rows = jnp.concatenate([near] + far, axis=0)
        scaled = (rows * share_ref[:, 0:1]).astype(jnp.bfloat16)
        held[:, part] = lax.dot_general(
            select, scaled, (((0,), (0,)), ((), ())), preferred_element_type=jnp.float32
        ).astype(jnp.bfloat16)
        copy = pltpu.make_async_copy(held.at[:, part], out_ref.at[:, part], sems.at[place])
        copy.start()
        copies.append(copy)
    for copy in copies:
        copy.wait()


def finish(select, share, nears, fars, capacity):
    flight = len(fars) + 1
    width = nears[0].shape[1]
    row_count = select.shape[1]
    places = width // column_step(width, 1024)
    return pl.pallas_call(
        functools.partial(finish_kernel, flight, capacity),
        out_shape=jax.ShapeDtypeStruct((row_count, width), jnp.bfloat16),
        in_specs=[VMEM] * (2 + len(nears) + len(fars)),
        out_specs=ANY,
        scratch_shapes=[
            pltpu.VMEM((row_count, width), jnp.bfloat16),
            pltpu.SemaphoreType.DMA((places,)),
        ],
        compiler_params=pltpu.CompilerParams(vmem_limit_bytes=16 << 20),
        cost_estimate=pl.CostEstimate(
            flops=2 * flight * capacity * row_count * width,
            bytes_accessed=2 * row_count * width,
            transcendentals=0,
        ),
        name="finish",
    )(select, share, *nears, *fars)


def local(
    tokens,
    group_choice,
    expert_picks,
    gate_fixed,
    token_counts,
    expert_gate,
    expert_up,
    expert_down,
):
    devices = lax.axis_size("node")
    flight = devices // SPLIT
    row_count = tokens.shape[0]
    capacity = row_count // 16
    me = (lax.axis_index("node") // SPLIT).astype(jnp.int32).reshape(1)

    def swap(array, bits):
        return lax.ppermute(array, "node", [(n, n ^ bits) for n in range(devices)])

    def shift(array, step):
        return lax.ppermute(
            array, "node", [(n, (n + step * SPLIT) % devices) for n in range(devices)]
        )

    gates = [expert_gate, swap(expert_gate, 1)]
    ups = [expert_up, swap(expert_up, 1)]
    downs = [expert_down, swap(expert_down, 1)]

    *rows, select, share = route(
        me, token_counts, group_choice.T, expert_picks.T, gate_fixed.T, tokens, flight, capacity
    )
    near = rows[0]
    far = [shift(rows[step], step) for step in range(1, flight)]
    far = far[0] if flight == 2 else jnp.concatenate(far, axis=0)

    nears = [near] + [swap(near, chip * CORES) for chip in range(1, CHIPS)]
    fars = [far] + [swap(far, chip * CORES) for chip in range(1, CHIPS)]

    near_parts = ffn(nears, gates, ups, downs)
    far_parts = ffn(fars, gates, ups, downs)

    far_back = [far_parts[0]] + [
        swap(far_parts[chip], chip * CORES) for chip in range(1, CHIPS)
    ]
    far_sum = far_back[0].astype(jnp.float32)
    for part in far_back[1:]:
        far_sum = far_sum + part.astype(jnp.float32)
    far_sum = far_sum.astype(jnp.bfloat16)
    far_home = [
        shift(far_sum[(step - 1) * capacity : step * capacity], -step)
        for step in range(1, flight)
    ]
    near_back = [near_parts[0]] + [
        swap(near_parts[chip], chip * CORES) for chip in range(1, CHIPS)
    ]
    return finish(select, share, near_back, far_home, capacity)


def solution(mesh):
    return jax.shard_map(
        local,
        mesh=mesh,
        in_specs=(
            P(("rep", "node"), None),
            P(("rep", "node"), None),
            P(("rep", "node"), None),
            P(("rep", "node"), None),
            P(("rep", "node")),
            P(None, "node"),
            P(None, "node"),
            P("node", None),
        ),
        out_specs=P(("rep", "node"), None),
        check_vma=False,
    )
```
